32 devices in a mesh: groups: 2 (over x), heads: 16 (over z, y, core).
Axes of the slice: x: 2, y: 2, z: 4, core: 2. Of those that a mesh axis runs over, the one named last changes fastest.
Arguments:
- tokens: bfloat16 [64, 4, 2304], P('groups'), parts along dimension 0, may hold values from -6 to 6
- qkv_weight: bfloat16 [4608, 12288], P(('groups', 'heads')), parts along dimension 0, may hold values from -0.125 to 0.125
- gate_weight: bfloat16 [4608, 64], P(('groups', 'heads')), parts along dimension 0, may hold values from -0.125 to 0.125
- conv_weight: bfloat16 [8, 12288], P('groups', 'heads'), parts along dimension 0, may hold values from -3 to 3
- delta_state: float32 [64, 32, 128, 128], P(('groups', 'heads')), parts along dimension 0, may hold values from -0.8 to 0.8
- conv_state: float32 [64, 3, 12288], P(('groups', 'heads')), parts along dimension 0, may hold values from -6 to 6
- old_heads: int32 [32], replicated, may hold values from 0 to 31, each once
- new_units: int32 [64], replicated, may hold values from 0 to 63, each once
- slot_of: int32 [64], P('groups'), parts along dimension 0, may hold values from 0 to 31, each once
- lengths: int32 [64], P('groups'), parts along dimension 0, may hold values from 1 to 4, as said below
Outputs:
- readout: bfloat16 [64, 4, 4096], P('groups', None, 'heads'), parts along dimension 0
The draws below stay inside these ranges and needn't reach their ends.
There are 2 independent parts, one for each index of `groups`. The reference program is written for one: setup_inputs(seed, part) draws one part's arguments, and reference() takes and returns one part's arrays. A program takes and returns all parts, laid end to end along the dimension named above; an argument that names none is the same for every part. Nothing has to cross between parts.
Inputs may be any that keep to these rules, and one draw needn't show every extreme that they name: `old_heads`: a permutation of the heads; old column slot p holds head old_heads[p]. `new_units`: a permutation of the head units; unit u is the half u % 2 of the values of head u // 2. `slot_of`: a permutation of the rows. `lengths`: some row decodes all 4 steps and some row only one.
All inputs are finite; a program needn't handle non-finite values.
Results may differ from the reference program's by a relative error of at most 0.001.
Values may be sent and summed in bfloat16 or wider, within the bound.
A program may use at most 128 MiB of HBM per device.

```python
import jax
import jax.numpy as jnp
from jax import lax

D = 2304
H = 32
DK = 128
TAPS = 4
STEPS = 4
ROLLOUTS = 32
HALF = 64
UNITS = 64


def draw_lengths(key, part):
    first_key, second_key = jax.random.split(key)
    values = jax.random.randint(first_key, (ROLLOUTS,), 1, STEPS + 1)
    spots = jax.random.permutation(second_key, ROLLOUTS)
    values = values.at[spots[0]].set(STEPS)
    values = values.at[spots[1]].set(1)
    return values.astype(jnp.int32)


def steps_of(rng, dims, shards, least, top_value):
    gain = 1.0
    for axis_at, shards_of in shards:
        heights = jax.random.uniform(jax.random.fold_in(jax.random.fold_in(rng, 6), axis_at), (shards_of,), jnp.float32, least / len(shards), top_value / len(shards))
        gain = gain * jnp.repeat(jnp.exp(heights), dims[axis_at] // shards_of).reshape((-1,) + (1,) * (len(dims) - 1 - axis_at))
    return gain


def bell_draw(own_key, shape, scale, bound, pieces=(), held_as=jnp.bfloat16):
    drawn = scale * jax.random.normal(own_key, shape, jnp.float32)
    if pieces:
        drawn = drawn * steps_of(own_key, shape, pieces, -0.22, 0.18)
    return jnp.clip(drawn, -bound, bound).astype(held_as)


def setup_inputs(seed: int = 0, part: int = 0) -> dict:
    streams_of = jax.random.split(jax.random.key(seed), 11)
    part_keys = jax.random.split(jax.random.fold_in(streams_of[10], part), 11)
    return {
        "tokens": bell_draw(part_keys[0], (ROLLOUTS, STEPS, D), 1.0, 6.0),
        "qkv_weight": bell_draw(part_keys[1], (D, 3 * H * DK), D ** -0.5, 0.125, ((0, 16),)),
        "gate_weight": bell_draw(part_keys[2], (D, 2 * H), D ** -0.5, 0.125, ((0, 16),)),
        "conv_weight": bell_draw(part_keys[3], (TAPS, 3 * H * DK), TAPS ** -0.5, 3.0, ((1, 16),)),
        "delta_state": bell_draw(part_keys[4], (ROLLOUTS, H, DK, DK), 0.1, 0.8, ((0, 16),), jnp.float32),
        "conv_state": bell_draw(part_keys[5], (ROLLOUTS, TAPS - 1, 3 * H * DK), 1.0, 6.0, ((0, 16),), jnp.float32),
        "old_heads": jax.random.permutation(streams_of[6], H).astype(jnp.int32),
        "new_units": jax.random.permutation(streams_of[7], UNITS).astype(jnp.int32),
        "slot_of": jax.random.permutation(part_keys[8], ROLLOUTS).astype(jnp.int32),
        "lengths": draw_lengths(jax.random.fold_in(jax.random.fold_in(streams_of[10], part), 71), part),
    }


norm_eps = 1e-06

def unit_tables(old_heads, new_units):
    positions = jnp.arange(H, dtype=jnp.int32)
    inverse = lax.optimization_barrier(jnp.sum(jnp.where(old_heads[None, :] == positions[:, None], positions[None, :], 0), axis=1)).astype(jnp.int32)
    heads_of = (new_units // 2).astype(jnp.int32)
    halves = (new_units % 2).astype(jnp.int32)
    old_slots = lax.optimization_barrier(jnp.sum(jnp.where(heads_of[:, None] == positions[None, :], inverse[None, :], 0), axis=1)).astype(jnp.int32)
    return (old_slots, halves)

def normalize(values):
    return values * jax.lax.rsqrt(lax.optimization_barrier(jnp.sum(values * values, axis=-1, keepdims=True)) + norm_eps)

def reference(tokens, qkv_weight, gate_weight, conv_weight, delta_state, conv_state, old_heads, new_units, slot_of, lengths):
    row_count = tokens.shape[0]
    flattened = tokens.reshape(row_count * STEPS, D)
    projected = jnp.dot(flattened, qkv_weight, preferred_element_type=jnp.float32).reshape(row_count, STEPS, 3 * H * DK)
    gate_logits = jnp.dot(flattened, gate_weight, preferred_element_type=jnp.float32).reshape(row_count, STEPS, 2, H)
    history = conv_state[slot_of]
    sequence = jnp.concatenate([history, projected], axis=1)
    tap_weights = conv_weight.astype(jnp.float32)
    convolved = tap_weights[0][None, None, :] * sequence[:, 0:STEPS]
    for tap_index in range(1, TAPS):
        convolved = convolved + tap_weights[tap_index][None, None, :] * sequence[:, tap_index:tap_index + STEPS]
    activated = jax.nn.silu(convolved).reshape(row_count, STEPS, 3, H, DK)
    queries = normalize(activated[:, :, 0])
    keys_all = normalize(activated[:, :, 1])
    values_all = activated[:, :, 2]
    beta = jax.nn.sigmoid(gate_logits[:, :, 0])
    decay = jnp.exp(-jax.nn.softplus(gate_logits[:, :, 1]))
    carried = delta_state[slot_of]
    readouts = []
    for step_index in range(STEPS):
        is_live = (step_index < lengths)[:, None, None, None]
        faded = decay[:, step_index, :, None, None] * carried
        predicted = lax.optimization_barrier(jnp.sum(keys_all[:, step_index, :, :, None] * faded, axis=2))
        updated = faded + beta[:, step_index, :, None, None] * keys_all[:, step_index, :, :, None] * (values_all[:, step_index] - predicted)[:, :, None, :]
        heads_now = lax.optimization_barrier(jnp.sum(queries[:, step_index, :, :, None] * updated, axis=2))
        carried = jnp.where(is_live, updated, carried)
        readouts.append(jnp.where(is_live[..., 0], heads_now, jnp.zeros_like(heads_now)))
    heads_out = jnp.stack(readouts, axis=1)
    old_slots, halves = unit_tables(old_heads, new_units)
    split_heads = heads_out.reshape(row_count, STEPS, H, 2, HALF)[:, :, old_slots]
    chosen = jnp.where((halves == 0)[None, None, :, None], split_heads[:, :, :, 0], split_heads[:, :, :, 1])
    return chosen.reshape(row_count, STEPS, UNITS * HALF).astype(jnp.bfloat16)
```

```python
import jax
import jax.numpy as jnp
from jax import lax
from jax.sharding import PartitionSpec as P

H = 32
DK = 128
TAPS = 4
STEPS = 4
HALF = 64
UNITS = 64
CHANNELS = 3 * H * DK

norm_eps = 1e-06


def unit_positions(old_heads, new_units):
    positions = jnp.arange(H, dtype=jnp.int32)
    inverse = jnp.sum(
        jnp.where(old_heads[None, :] == positions[:, None], positions[None, :], 0), axis=1
    )
    heads_of = new_units // 2
    old_slots = jnp.sum(
        jnp.where(heads_of[:, None] == positions[None, :], inverse[None, :], 0), axis=1
    )
    return old_slots * 2 + new_units % 2


def normalize(values):
    return values * lax.rsqrt(jnp.sum(values * values, axis=-1, keepdims=True) + norm_eps)


def decode(projected, gate_pre, history, taps, state, live_lengths):
    rows = projected.shape[0]
    sequence = jnp.concatenate([history, projected], axis=1)
    weights_f = taps.astype(jnp.float32)
    convolved = weights_f[0][None, None] * sequence[:, 0:STEPS]
    for tap_index in range(1, TAPS):
        convolved = (
            convolved
            + weights_f[tap_index][None, None] * sequence[:, tap_index : tap_index + STEPS]
        )
    activated = jax.nn.silu(convolved).reshape(rows, STEPS, 3, H, DK)
    queries = normalize(activated[:, :, 0])
    keys = normalize(activated[:, :, 1])
    values = activated[:, :, 2]
    beta = jax.nn.sigmoid(gate_pre[:, :, 0])
    decay = jnp.exp(-jax.nn.softplus(gate_pre[:, :, 1]))
    both = jnp.concatenate([queries, keys], axis=1)
    based = jnp.einsum("rihk,rhkv->rihv", both, state, precision=lax.Precision.HIGHEST)
    query_base, key_base = based[:, :STEPS], based[:, STEPS:]

    corrections = []
    outs = []
    faded_base = jnp.ones_like(decay[:, 0])
    spans = []
    for s in range(STEPS):
        faded_base = faded_base * decay[:, s]
        spans = [span * decay[:, s] for span in spans]
        predicted = faded_base[..., None] * key_base[:, s]
        for j in range(s):
            overlap = jnp.sum(keys[:, s] * keys[:, j], axis=-1) * spans[j]
            predicted = predicted + overlap[..., None] * corrections[j]
        corrections.append(beta[:, s, :, None] * (values[:, s] - predicted))
        spans.append(jnp.ones_like(faded_base))
        now = faded_base[..., None] * query_base[:, s]
        for j in range(s + 1):
            overlap = jnp.sum(queries[:, s] * keys[:, j], axis=-1) * spans[j]
            now = now + overlap[..., None] * corrections[j]
        live = (s < live_lengths)[:, None, None]
        outs.append(jnp.where(live, now, jnp.zeros_like(now)))
    return jnp.stack(outs, axis=1).astype(jnp.bfloat16)


def on_device(
    tokens,
    qkv_weight,
    gate_weight,
    conv_weight,
    delta_state,
    conv_state,
    old_heads,
    new_units,
    slot_of,
    lengths,
):
    devices = lax.axis_size("heads")
    my_index = lax.axis_index("heads")
    row_count = tokens.shape[0]
    rows_dev = delta_state.shape[0]
    depth = qkv_weight.shape[0]
    taps = lax.all_gather(conv_weight, "heads", axis=1, tiled=True)

    row_range = jnp.arange(row_count, dtype=jnp.int32)
    to_old = (slot_of[None, :] == row_range[:, None]).astype(jnp.bfloat16)
    tokens_old = jnp.einsum(
        "ob,bsd->osd", to_old, tokens, preferred_element_type=jnp.float32
    ).astype(jnp.bfloat16)
    width = tokens.shape[2]
    columns = H * DK // devices
    shaped = qkv_weight.reshape(depth, 3, devices, columns)
    mine_weight = lax.all_to_all(shaped, "heads", split_axis=2, concat_axis=0, tiled=True)
    projected_all = jnp.dot(
        tokens_old.reshape(row_count * STEPS, width),
        mine_weight.reshape(width, 3 * columns),
        preferred_element_type=jnp.float32,
    ).reshape(row_count, STEPS, 3, 1, columns)
    projected = lax.all_to_all(
        projected_all, "heads", split_axis=0, concat_axis=3, tiled=True
    ).reshape(rows_dev, STEPS, CHANNELS)
    gates_all = lax.all_gather(gate_weight, "heads", axis=0, tiled=True)
    my_tokens = lax.dynamic_slice_in_dim(tokens_old, my_index * rows_dev, rows_dev, 0)
    gate_pre = jnp.dot(
        my_tokens.reshape(rows_dev * STEPS, width), gates_all, preferred_element_type=jnp.float32
    ).reshape(rows_dev, STEPS, 2, H)

    my_slots = my_index * rows_dev + jnp.arange(rows_dev, dtype=jnp.int32)
    live_lengths = jnp.sum(
        jnp.where(slot_of[None, :] == my_slots[:, None], lengths[None, :], 0), axis=1
    )
    heads_out = decode(projected, gate_pre, conv_state, taps, delta_state, live_lengths)

    unit_from = unit_positions(old_heads, new_units)
    pick = (unit_from[:, None] == jnp.arange(UNITS, dtype=jnp.int32)[None, :]).astype(jnp.bfloat16)
    units_out = jnp.einsum(
        "rsxc,ux->rsuc",
        heads_out.reshape(rows_dev, STEPS, UNITS, HALF),
        pick,
        preferred_element_type=jnp.float32,
    ).astype(jnp.bfloat16)
    outputs_old = lax.all_to_all(units_out, "heads", split_axis=2, concat_axis=0, tiled=True)
    flat_old = outputs_old.reshape(row_count, STEPS, (UNITS // devices) * HALF)
    return jnp.einsum(
        "ob,osc->bsc", to_old, flat_old, preferred_element_type=jnp.float32
    ).astype(jnp.bfloat16)


def solution(mesh):
    in_specs = (
        P("groups", None, None),
        P(("groups", "heads"), None),
        P(("groups", "heads"), None),
        P("groups", "heads"),
        P(("groups", "heads"), None, None, None),
        P(("groups", "heads"), None, None),
        P(),
        P(),
        P("groups"),
        P("groups"),
    )
    return jax.shard_map(
        on_device,
        mesh=mesh,
        in_specs=in_specs,
        out_specs=P("groups", None, "heads"),
        check_vma=False,
    )
```

```python
import functools

import jax
import jax.numpy as jnp
from jax import lax
from jax.experimental import pallas as pl
from jax.experimental.pallas import tpu as pltpu
from jax.sharding import PartitionSpec as P

H = 32
DK = 128
TAPS = 4
STEPS = 4
HALF = 64
UNITS = 64
CHANNELS = 3 * H * DK

GROUP = 4
SPAN = H * DK // GROUP
CHUNK = 512
PER_SPAN = SPAN // CHUNK
CHUNKS = 3 * PER_SPAN
LAG = 2

norm_eps = 1e-06


def project_kernel(
    devices,
    rows,
    w_ref,
    gate_ref,
    tap_ref,
    toks_ref,
    out_ref,
    gate_out_ref,
    tap_out_ref,
    land,
    partial,
    red,
    summed,
    final,
    gate_land,
    gate_partial,
    gate_red,
    tap_land,
    own_sem,
    w_send,
    w_recv,
    z_send,
    z_recv,
    f_send,
    f_recv,
    g_send,
    g_recv,
    h_send,
    h_recv,
    t_send,
    t_recv,
):
    me = lax.axis_index("heads")
    outer = devices // GROUP
    place, inner = me // GROUP, me % GROUP
    band = GROUP * rows

    def remote(src, dst, send, recv, target):
        return pltpu.make_async_remote_copy(
            src_ref=src,
            dst_ref=dst,
            send_sem=send,
            recv_sem=recv,
            device_id={"heads": target},
            device_id_type=pl.DeviceIdType.MESH,
        )

    def mate(k):
        return place * GROUP + (inner + k) % GROUP

    def across(k):
        return ((place + k) % outer) * GROUP + inner

    def source_columns(c, owner):
        start = (c // PER_SPAN) * H * DK + owner * SPAN + (c % PER_SPAN) * CHUNK
        return pl.ds(pl.multiple_of(start, CHUNK), CHUNK)

    def local_columns(c):
        return pl.ds(c * CHUNK, CHUNK)

    own = []
    for c in range(CHUNKS):
        own.append(
            pltpu.make_async_copy(
                w_ref.at[:, source_columns(c, inner)],
                land.at[0, :, local_columns(c)],
                own_sem.at[c],
            )
        )
        own[c].start()

    barrier = pltpu.get_barrier_semaphore()
    for k in range(1, devices):
        pl.semaphore_signal(
            barrier,
            inc=1,
            device_id={"heads": (me + k) % devices},
            device_id_type=pl.DeviceIdType.MESH,
        )
    pl.semaphore_wait(barrier, devices - 1)

    gates = []
    for k in range(1, GROUP):
        gates.append(
            remote(gate_ref, gate_land.at[k - 1], g_send.at[k - 1], g_recv.at[k - 1], mate(k))
        )
        gates[-1].start()
    spread = []
    for c in range(CHUNKS):
        group = []
        for k in range(1, GROUP):
            owner = (inner + k) % GROUP
            group.append(
                remote(
                    w_ref.at[:, source_columns(c, owner)],
                    land.at[k, :, local_columns(c)],
                    w_send.at[c, k - 1],
                    w_recv.at[c, k - 1],
                    mate(k),
                )
            )
            group[-1].start()
        spread.append(group)
        if c == 0:
            taps = []
            for k in range(1, devices):
                taps.append(
                    remote(
                        tap_ref,
                        tap_land.at[me],
                        t_send.at[k - 1],
                        t_recv.at[k - 1],
                        (me + k) % devices,
                    )
                )
                taps[-1].start()

    for copy in gates:
        copy.wait()
    total = jnp.dot(toks_ref[inner], gate_ref[...], preferred_element_type=jnp.float32)
    for k in range(1, GROUP):
        source = (inner + GROUP - k) % GROUP
        total = total + jnp.dot(
            toks_ref[source], gate_land[k - 1], preferred_element_type=jnp.float32
        )
    gate_partial[...] = total
    gate_sends = []
    for k in range(1, outer):
        start = ((place + k) % outer) * band + inner * rows
        gate_sends.append(
            remote(
                gate_partial.at[pl.ds(pl.multiple_of(start, rows), rows)],
                gate_red.at[k - 1],
                h_send.at[k - 1],
                h_recv.at[k - 1],
                across(k),
            )
        )
        gate_sends[-1].start()

    my_band = pl.ds(pl.multiple_of(place * band, band), band)
    crossing = []
    closing = []

    def finish(c):
        here = local_columns(c)
        for copy in crossing[c]:
            copy.wait()
        whole = partial[my_band, here]
        for k in range(1, outer):
            whole = whole + red[k - 1, :, here]
        summed[:, here] = whole
        group = []
        for k in range(1, GROUP):
            start = ((inner + k) % GROUP) * rows
            group.append(
                remote(
                    summed.at[pl.ds(pl.multiple_of(start, rows), rows), here],
                    final.at[k - 1, :, here],
                    f_send.at[c, k - 1],
                    f_recv.at[c, k - 1],
                    mate(k),
                )
            )
            group[-1].start()
        closing.append(group)

    for c in range(CHUNKS):
        here = local_columns(c)
        own[c].wait()
        for copy in spread[c]:
            copy.wait_recv()
        total = jnp.dot(toks_ref[inner], land[0, :, here], preferred_element_type=jnp.float32)
        for k in range(1, GROUP):
            source = (inner + GROUP - k) % GROUP
            total = total + jnp.dot(
                toks_ref[source], land[k, :, here], preferred_element_type=jnp.float32
            )
        partial[:, here] = total
        group = []
        for k in range(1, outer):
            start = ((place + k) % outer) * band
            group.append(
                remote(
                    partial.at[pl.ds(pl.multiple_of(start, band), band), here],
                    red.at[k - 1, :, here],
                    z_send.at[c, k - 1],
                    z_recv.at[c, k - 1],
                    across(k),
                )
            )
            group[-1].start()
        crossing.append(group)
        if c >= LAG:
            finish(c - LAG)
    for c in range(CHUNKS - LAG, CHUNKS):
        finish(c)

    for copy in gate_sends:
        copy.wait()
    my_rows = pl.ds(pl.multiple_of(me * rows, rows), rows)
    gate_total = gate_partial[my_rows, :]
    for k in range(1, outer):
        gate_total = gate_total + gate_red[k - 1]
    gate_out_ref[...] = gate_total
    for copy in taps:
        copy.wait()
    tap_land[me] = tap_ref[...]
    tap_out_ref[...] = tap_land[...]
    kept = pl.ds(pl.multiple_of(inner * rows, rows), rows)
    for c in range(CHUNKS):
        here = local_columns(c)
        out_ref[:, source_columns(c, inner)] = summed[kept, here]
        for k in range(1, GROUP):
            closing[c][k - 1].wait()
            source = (inner + GROUP - k) % GROUP
            out_ref[:, source_columns(c, source)] = final[k - 1, :, here]
    for group in spread:
        for copy in group:
            copy.wait_send()


def project(devices, rows, weight, gate, taps, toks):
    depth = weight.shape[0]
    outer = devices // GROUP
    total = devices * rows
    band = GROUP * rows
    dma = pltpu.SemaphoreType.DMA
    vmem = pl.BlockSpec(memory_space=pltpu.VMEM)
    return pl.pallas_call(
        functools.partial(project_kernel, devices, rows),
        out_shape=(
            jax.ShapeDtypeStruct((rows, CHANNELS), jnp.float32),
            jax.ShapeDtypeStruct((rows, gate.shape[1]), jnp.float32),
            jax.ShapeDtypeStruct((devices,) + taps.shape, taps.dtype),
        ),
        in_specs=[pl.BlockSpec(memory_space=pl.ANY), vmem, vmem, vmem],
        out_specs=(vmem, vmem, vmem),
        scratch_shapes=[
            pltpu.VMEM((GROUP, depth, 3 * SPAN), jnp.bfloat16),
            pltpu.VMEM((total, 3 * SPAN), jnp.float32),
            pltpu.VMEM((outer - 1, band, 3 * SPAN), jnp.float32),
            pltpu.VMEM((band, 3 * SPAN), jnp.float32),
            pltpu.VMEM((GROUP - 1, rows, 3 * SPAN), jnp.float32),
            pltpu.VMEM((GROUP - 1,) + gate.shape, jnp.bfloat16),
            pltpu.VMEM((total, gate.shape[1]), jnp.float32),
            pltpu.VMEM((outer - 1, rows, gate.shape[1]), jnp.float32),
            pltpu.VMEM((devices,) + taps.shape, taps.dtype),
            dma((CHUNKS,)),
            dma((CHUNKS, GROUP - 1)),
            dma((CHUNKS, GROUP - 1)),
            dma((CHUNKS, outer - 1)),
            dma((CHUNKS, outer - 1)),
            dma((CHUNKS, GROUP - 1)),
            dma((CHUNKS, GROUP - 1)),
            dma((GROUP - 1,)),
            dma((GROUP - 1,)),
            dma((outer - 1,)),
            dma((outer - 1,)),
            dma((devices - 1,)),
            dma((devices - 1,)),
        ],
        compiler_params=pltpu.CompilerParams(
            collective_id=0, has_side_effects=True, vmem_limit_bytes=48 * 1024 * 1024
        ),
    )(weight, gate, taps, toks)


def unit_positions(old_heads, new_units):
    positions = jnp.arange(H, dtype=jnp.int32)
    inverse = jnp.sum(
        jnp.where(old_heads[None, :] == positions[:, None], positions[None, :], 0), axis=1
    )
    heads_of = new_units // 2
    old_slots = jnp.sum(
        jnp.where(heads_of[:, None] == positions[None, :], inverse[None, :], 0), axis=1
    )
    return old_slots * 2 + new_units % 2


def normalize(values):
    return values * lax.rsqrt(jnp.sum(values * values, axis=-1, keepdims=True) + norm_eps)


def decode(projected, gate_pre, history, taps, state, live_lengths):
    rows = projected.shape[0]
    sequence = jnp.concatenate([history, projected], axis=1)
    weights_f = taps.astype(jnp.float32)
    convolved = weights_f[0][None, None] * sequence[:, 0:STEPS]
    for tap_index in range(1, TAPS):
        convolved = (
            convolved
            + weights_f[tap_index][None, None] * sequence[:, tap_index : tap_index + STEPS]
        )
    activated = jax.nn.silu(convolved).reshape(rows, STEPS, 3, H, DK)
    queries = normalize(activated[:, :, 0])
    keys = normalize(activated[:, :, 1])
    values = activated[:, :, 2]
    beta = jax.nn.sigmoid(gate_pre[:, :, 0])
    decay = jnp.exp(-jax.nn.softplus(gate_pre[:, :, 1]))
    both = jnp.concatenate([queries, keys], axis=1)
    based = jnp.einsum("rihk,rhkv->rihv", both, state, precision=lax.Precision.HIGHEST)
    query_base, key_base = based[:, :STEPS], based[:, STEPS:]

    corrections = []
    outs = []
    faded_base = jnp.ones_like(decay[:, 0])
    spans = []
    for s in range(STEPS):
        faded_base = faded_base * decay[:, s]
        spans = [span * decay[:, s] for span in spans]
        predicted = faded_base[..., None] * key_base[:, s]
        for j in range(s):
            overlap = jnp.sum(keys[:, s] * keys[:, j], axis=-1) * spans[j]
            predicted = predicted + overlap[..., None] * corrections[j]
        corrections.append(beta[:, s, :, None] * (values[:, s] - predicted))
        spans.append(jnp.ones_like(faded_base))
        now = faded_base[..., None] * query_base[:, s]
        for j in range(s + 1):
            overlap = jnp.sum(queries[:, s] * keys[:, j], axis=-1) * spans[j]
            now = now + overlap[..., None] * corrections[j]
        live = (s < live_lengths)[:, None, None]
        outs.append(jnp.where(live, now, jnp.zeros_like(now)))
    return jnp.stack(outs, axis=1).astype(jnp.bfloat16)


def on_device(
    tokens,
    qkv_weight,
    gate_weight,
    conv_weight,
    delta_state,
    conv_state,
    old_heads,
    new_units,
    slot_of,
    lengths,
):
    devices = lax.axis_size("heads")
    my_index = lax.axis_index("heads")
    row_count = tokens.shape[0]
    rows_dev = delta_state.shape[0]
    depth = qkv_weight.shape[0]
    row_range = jnp.arange(row_count, dtype=jnp.int32)
    to_old = (slot_of[None, :] == row_range[:, None]).astype(jnp.bfloat16)
    tokens_old = jnp.einsum(
        "ob,bsd->osd", to_old, tokens, preferred_element_type=jnp.float32
    ).astype(jnp.bfloat16)
    rows = rows_dev * STEPS
    place = my_index // GROUP
    toks = lax.dynamic_slice_in_dim(
        tokens_old.reshape(row_count * STEPS, tokens.shape[2]),
        place * GROUP * depth,
        GROUP * depth,
        1,
    )
    toks = toks.reshape(row_count * STEPS, GROUP, depth).transpose(1, 0, 2)
    gate_padded = jnp.pad(gate_weight, ((0, 0), (0, 128 - 2 * H)))
    tap_padded = jnp.pad(conv_weight, ((0, 16 - TAPS), (0, 0)))
    mine, gate_mine, tap_table = project(devices, rows, qkv_weight, gate_padded, tap_padded, toks)
    projected = mine.reshape(rows_dev, STEPS, CHANNELS)
    gate_pre = gate_mine[:, : 2 * H].reshape(rows_dev, STEPS, 2, H)
    taps = tap_table[:, :TAPS].transpose(1, 0, 2).reshape(TAPS, CHANNELS)

    my_slots = my_index * rows_dev + jnp.arange(rows_dev, dtype=jnp.int32)
    live_lengths = jnp.sum(
        jnp.where(slot_of[None, :] == my_slots[:, None], lengths[None, :], 0), axis=1
    )
    heads_out = decode(projected, gate_pre, conv_state, taps, delta_state, live_lengths)

    unit_from = unit_positions(old_heads, new_units)
    pick = (unit_from[:, None] == jnp.arange(UNITS, dtype=jnp.int32)[None, :]).astype(jnp.bfloat16)
    units_out = jnp.einsum(
        "rsxc,ux->rsuc",
        heads_out.reshape(rows_dev, STEPS, UNITS, HALF),
        pick,
        preferred_element_type=jnp.float32,
    ).astype(jnp.bfloat16)
    outputs_old = lax.all_to_all(units_out, "heads", split_axis=2, concat_axis=0, tiled=True)
    flat_old = outputs_old.reshape(row_count, STEPS, (UNITS // devices) * HALF)
    return jnp.einsum(
        "ob,osc->bsc", to_old, flat_old, preferred_element_type=jnp.float32
    ).astype(jnp.bfloat16)


def solution(mesh):
    in_specs = (
        P("groups", None, None),
        P(("groups", "heads"), None),
        P(("groups", "heads"), None),
        P("groups", "heads"),
        P(("groups", "heads"), None, None, None),
        P(("groups", "heads"), None, None),
        P(),
        P(),
        P("groups"),
        P("groups"),
    )
    return jax.shard_map(
        on_device,
        mesh=mesh,
        in_specs=in_specs,
        out_specs=P("groups", None, "heads"),
        check_vma=False,
    )
```

```python
import functools

import jax
import jax.numpy as jnp
from jax import lax
from jax.experimental import pallas as pl
from jax.experimental.pallas import tpu as pltpu
from jax.sharding import PartitionSpec as P

H = 32
DK = 128
TAPS = 4
STEPS = 4
HALF = 64
UNITS = 64
CHANNELS = 3 * H * DK

GROUP = 4
SPAN = H * DK // GROUP
CHUNK = 256
PER_SPAN = SPAN // CHUNK
CHUNKS = 3 * PER_SPAN
LAG = 2

norm_eps = 1e-06


def project_kernel(
    devices,
    rows,
    w_ref,
    gate_ref,
    tap_ref,
    toks_ref,
    out_ref,
    gate_out_ref,
    tap_out_ref,
    land,
    partial,
    red,
    summed,
    final,
    gate_land,
    gate_partial,
    gate_red,
    tap_land,
    own_sem,
    w_send,
    w_recv,
    z_send,
    z_recv,
    f_send,
    f_recv,
    g_send,
    g_recv,
    h_send,
    h_recv,
    t_send,
    t_recv,
):
    me = lax.axis_index("heads")
    outer = devices // GROUP
    place, inner = me // GROUP, me % GROUP
    band = GROUP * rows

    def remote(src, dst, send, recv, target):
        return pltpu.make_async_remote_copy(
            src_ref=src,
            dst_ref=dst,
            send_sem=send,
            recv_sem=recv,
            device_id={"heads": target},
            device_id_type=pl.DeviceIdType.MESH,
        )

    def mate(k):
        return place * GROUP + (inner + k) % GROUP

    def across(k):
        return ((place + k) % outer) * GROUP + inner

    def source_columns(c, owner):
        start = (c // PER_SPAN) * H * DK + owner * SPAN + (c % PER_SPAN) * CHUNK
        return pl.ds(pl.multiple_of(start, CHUNK), CHUNK)

    def local_columns(c):
        return pl.ds(c * CHUNK, CHUNK)

    own = []
    for c in range(CHUNKS):
        own.append(
            pltpu.make_async_copy(
                w_ref.at[:, source_columns(c, inner)],
                land.at[0, :, local_columns(c)],
                own_sem.at[c],
            )
        )
        own[c].start()

    barrier = pltpu.get_barrier_semaphore()
    for k in range(1, devices):
        pl.semaphore_signal(
            barrier,
            inc=1,
            device_id={"heads": (me + k) % devices},
            device_id_type=pl.DeviceIdType.MESH,
        )
    pl.semaphore_wait(barrier, devices - 1)

    gates = []
    for k in range(1, GROUP):
        gates.append(
            remote(gate_ref, gate_land.at[k - 1], g_send.at[k - 1], g_recv.at[k - 1], mate(k))
        )
        gates[-1].start()
    spread = []
    for c in range(CHUNKS):
        group = []
        for k in range(1, GROUP):
            owner = (inner + k) % GROUP
            group.append(
                remote(
                    w_ref.at[:, source_columns(c, owner)],
                    land.at[k, :, local_columns(c)],
                    w_send.at[c, k - 1],
                    w_recv.at[c, k - 1],
                    mate(k),
                )
            )
            group[-1].start()
        spread.append(group)
        if c == 0:
            taps = []
            for k in range(1, devices):
                taps.append(
                    remote(
                        tap_ref,
                        tap_land.at[me],
                        t_send.at[k - 1],
                        t_recv.at[k - 1],
                        (me + k) % devices,
                    )
                )
                taps[-1].start()

    for copy in gates:
        copy.wait()
    total = jnp.dot(toks_ref[inner], gate_ref[...], preferred_element_type=jnp.float32)
    for k in range(1, GROUP):
        source = (inner + GROUP - k) % GROUP
        total = total + jnp.dot(
            toks_ref[source], gate_land[k - 1], preferred_element_type=jnp.float32
        )
    gate_partial[...] = total
    gate_sends = []
    for k in range(1, outer):
        start = ((place + k) % outer) * band + inner * rows
        gate_sends.append(
            remote(
                gate_partial.at[pl.ds(pl.multiple_of(start, rows), rows)],
                gate_red.at[k - 1],
                h_send.at[k - 1],
                h_recv.at[k - 1],
                across(k),
            )
        )
        gate_sends[-1].start()

    my_band = pl.ds(pl.multiple_of(place * band, band), band)
    crossing = []
    closing = []

    def finish(c):
        here = local_columns(c)
        for copy in crossing[c]:
            copy.wait()
        whole = partial[my_band, here]
        for k in range(1, outer):
            whole = whole + red[k - 1, :, here]
        summed[:, here] = whole
        group = []
        for k in range(1, GROUP):
            start = ((inner + k) % GROUP) * rows
            group.append(
                remote(
                    summed.at[pl.ds(pl.multiple_of(start, rows), rows), here],
                    final.at[k - 1, :, here],
                    f_send.at[c, k - 1],
                    f_recv.at[c, k - 1],
                    mate(k),
                )
            )
            group[-1].start()
        closing.append(group)

    for c in range(CHUNKS):
        here = local_columns(c)
        own[c].wait()
        for copy in spread[c]:
            copy.wait_recv()
        total = jnp.dot(toks_ref[inner], land[0, :, here], preferred_element_type=jnp.float32)
        for k in range(1, GROUP):
            source = (inner + GROUP - k) % GROUP
            total = total + jnp.dot(
                toks_ref[source], land[k, :, here], preferred_element_type=jnp.float32
            )
        partial[:, here] = total
        group = []
        for k in range(1, outer):
            start = ((place + k) % outer) * band
            group.append(
                remote(
                    partial.at[pl.ds(pl.multiple_of(start, band), band), here],
                    red.at[k - 1, :, here],
                    z_send.at[c, k - 1],
                    z_recv.at[c, k - 1],
                    across(k),
                )
            )
            group[-1].start()
        crossing.append(group)
        if c >= LAG:
            finish(c - LAG)
    for c in range(CHUNKS - LAG, CHUNKS):
        finish(c)

    for copy in gate_sends:
        copy.wait()
    my_rows = pl.ds(pl.multiple_of(me * rows, rows), rows)
    gate_total = gate_partial[my_rows, :]
    for k in range(1, outer):
        gate_total = gate_total + gate_red[k - 1]
    gate_out_ref[...] = gate_total
    for copy in taps:
        copy.wait()
    tap_land[me] = tap_ref[...]
    tap_out_ref[...] = tap_land[...]
    kept = pl.ds(pl.multiple_of(inner * rows, rows), rows)
    for c in range(CHUNKS):
        here = local_columns(c)
        out_ref[:, source_columns(c, inner)] = summed[kept, here]
        for k in range(1, GROUP):
            closing[c][k - 1].wait()
            source = (inner + GROUP - k) % GROUP
            out_ref[:, source_columns(c, source)] = final[k - 1, :, here]
    for group in spread:
        for copy in group:
            copy.wait_send()


def project(devices, rows, weight, gate, taps, toks):
    depth = weight.shape[0]
    outer = devices // GROUP
    total = devices * rows
    band = GROUP * rows
    dma = pltpu.SemaphoreType.DMA
    vmem = pl.BlockSpec(memory_space=pltpu.VMEM)
    return pl.pallas_call(
        functools.partial(project_kernel, devices, rows),
        out_shape=(
            jax.ShapeDtypeStruct((rows, CHANNELS), jnp.float32),
            jax.ShapeDtypeStruct((rows, gate.shape[1]), jnp.float32),
            jax.ShapeDtypeStruct((devices,) + taps.shape, taps.dtype),
        ),
        in_specs=[pl.BlockSpec(memory_space=pl.ANY), vmem, vmem, vmem],
        out_specs=(vmem, vmem, vmem),
        scratch_shapes=[
            pltpu.VMEM((GROUP, depth, 3 * SPAN), jnp.bfloat16),
            pltpu.VMEM((total, 3 * SPAN), jnp.float32),
            pltpu.VMEM((outer - 1, band, 3 * SPAN), jnp.float32),
            pltpu.VMEM((band, 3 * SPAN), jnp.float32),
            pltpu.VMEM((GROUP - 1, rows, 3 * SPAN), jnp.float32),
            pltpu.VMEM((GROUP - 1,) + gate.shape, jnp.bfloat16),
            pltpu.VMEM((total, gate.shape[1]), jnp.float32),
            pltpu.VMEM((outer - 1, rows, gate.shape[1]), jnp.float32),
            pltpu.VMEM((devices,) + taps.shape, taps.dtype),
            dma((CHUNKS,)),
            dma((CHUNKS, GROUP - 1)),
            dma((CHUNKS, GROUP - 1)),
            dma((CHUNKS, outer - 1)),
            dma((CHUNKS, outer - 1)),
            dma((CHUNKS, GROUP - 1)),
            dma((CHUNKS, GROUP - 1)),
            dma((GROUP - 1,)),
            dma((GROUP - 1,)),
            dma((outer - 1,)),
            dma((outer - 1,)),
            dma((devices - 1,)),
            dma((devices - 1,)),
        ],
        compiler_params=pltpu.CompilerParams(
            collective_id=0, has_side_effects=True, vmem_limit_bytes=48 * 1024 * 1024
        ),
    )(weight, gate, taps, toks)


def exchange_kernel(devices, blocks_ref, out_ref, land, send, recv):
    me = lax.axis_index("heads")
    barrier = pltpu.get_barrier_semaphore()
    for k in range(1, devices):
        pl.semaphore_signal(
            barrier,
            inc=1,
            device_id={"heads": (me + k) % devices},
            device_id_type=pl.DeviceIdType.MESH,
        )
    pl.semaphore_wait(barrier, devices - 1)
    copies = []
    for k in range(1, devices):
        target = (me + k) % devices
        copies.append(
            pltpu.make_async_remote_copy(
                src_ref=blocks_ref.at[target],
                dst_ref=land.at[me],
                send_sem=send.at[k - 1],
                recv_sem=recv.at[k - 1],
                device_id={"heads": target},
                device_id_type=pl.DeviceIdType.MESH,
            )
        )
        copies[-1].start()
    land[me] = blocks_ref[me]
    for copy in copies:
        copy.wait()
    out_ref[...] = land[...]


def exchange(devices, blocks):
    vmem = pl.BlockSpec(memory_space=pltpu.VMEM)
    return pl.pallas_call(
        functools.partial(exchange_kernel, devices),
        out_shape=jax.ShapeDtypeStruct(blocks.shape, blocks.dtype),
        in_specs=[vmem],
        out_specs=vmem,
        scratch_shapes=[
            pltpu.VMEM(blocks.shape, blocks.dtype),
            pltpu.SemaphoreType.DMA((devices - 1,)),
            pltpu.SemaphoreType.DMA((devices - 1,)),
        ],
        compiler_params=pltpu.CompilerParams(collective_id=1, has_side_effects=True),
    )(blocks)


def unit_positions(old_heads, new_units):
    positions = jnp.arange(H, dtype=jnp.int32)
    inverse = jnp.sum(
        jnp.where(old_heads[None, :] == positions[:, None], positions[None, :], 0), axis=1
    )
    heads_of = new_units // 2
    old_slots = jnp.sum(
        jnp.where(heads_of[:, None] == positions[None, :], inverse[None, :], 0), axis=1
    )
    return old_slots * 2 + new_units % 2


def normalize(values):
    return values * lax.rsqrt(jnp.sum(values * values, axis=-1, keepdims=True) + norm_eps)


def decode(projected, gate_pre, history, taps, state, live_lengths):
    rows = projected.shape[0]
    sequence = jnp.concatenate([history, projected], axis=1)
    weights_f = taps.astype(jnp.float32)
    convolved = weights_f[0][None, None] * sequence[:, 0:STEPS]
    for tap_index in range(1, TAPS):
        convolved = (
            convolved
            + weights_f[tap_index][None, None] * sequence[:, tap_index : tap_index + STEPS]
        )
    activated = jax.nn.silu(convolved).reshape(rows, STEPS, 3, H, DK)
    queries = normalize(activated[:, :, 0])
    keys = normalize(activated[:, :, 1])
    values = activated[:, :, 2]
    beta = jax.nn.sigmoid(gate_pre[:, :, 0])
    decay = jnp.exp(-jax.nn.softplus(gate_pre[:, :, 1]))
    both = jnp.concatenate([queries, keys], axis=1)
    based = jnp.einsum("rihk,rhkv->rihv", both, state, precision=lax.Precision.HIGH)
    query_base, key_base = based[:, :STEPS], based[:, STEPS:]

    corrections = []
    outs = []
    faded_base = jnp.ones_like(decay[:, 0])
    spans = []
    for s in range(STEPS):
        faded_base = faded_base * decay[:, s]
        spans = [span * decay[:, s] for span in spans]
        predicted = faded_base[..., None] * key_base[:, s]
        for j in range(s):
            overlap = jnp.sum(keys[:, s] * keys[:, j], axis=-1) * spans[j]
            predicted = predicted + overlap[..., None] * corrections[j]
        corrections.append(beta[:, s, :, None] * (values[:, s] - predicted))
        spans.append(jnp.ones_like(faded_base))
        now = faded_base[..., None] * query_base[:, s]
        for j in range(s + 1):
            overlap = jnp.sum(queries[:, s] * keys[:, j], axis=-1) * spans[j]
            now = now + overlap[..., None] * corrections[j]
        live = (s < live_lengths)[:, None, None]
        outs.append(jnp.where(live, now, jnp.zeros_like(now)))
    return jnp.stack(outs, axis=1).astype(jnp.bfloat16)


def on_device(
    tokens,
    qkv_weight,
    gate_weight,
    conv_weight,
    delta_state,
    conv_state,
    old_heads,
    new_units,
    slot_of,
    lengths,
):
    devices = lax.axis_size("heads")
    my_index = lax.axis_index("heads")
    row_count = tokens.shape[0]
    rows_dev = delta_state.shape[0]
    depth = qkv_weight.shape[0]
    row_range = jnp.arange(row_count, dtype=jnp.int32)
    to_old = (slot_of[None, :] == row_range[:, None]).astype(jnp.bfloat16)
    rows = rows_dev * STEPS
    place = my_index // GROUP
    my_tokens = lax.dynamic_slice_in_dim(tokens, place * GROUP * depth, GROUP * depth, 2)
    tokens_old = jnp.einsum(
        "ob,bsd->osd", to_old, my_tokens, preferred_element_type=jnp.float32
    ).astype(jnp.bfloat16)
    toks = tokens_old.reshape(row_count * STEPS, GROUP, depth).transpose(1, 0, 2)
    gate_padded = jnp.pad(gate_weight, ((0, 0), (0, 128 - 2 * H)))
    tap_padded = jnp.pad(conv_weight, ((0, 16 - TAPS), (0, 0)))
    mine, gate_mine, tap_table = project(devices, rows, qkv_weight, gate_padded, tap_padded, toks)
    projected = mine.reshape(rows_dev, STEPS, CHANNELS)
    gate_pre = gate_mine[:, : 2 * H].reshape(rows_dev, STEPS, 2, H)
    taps = tap_table[:, :TAPS].transpose(1, 0, 2).reshape(TAPS, CHANNELS)

    my_slots = my_index * rows_dev + jnp.arange(rows_dev, dtype=jnp.int32)
    live_lengths = jnp.sum(
        jnp.where(slot_of[None, :] == my_slots[:, None], lengths[None, :], 0), axis=1
    )
    heads_out = decode(projected, gate_pre, conv_state, taps, delta_state, live_lengths)

    unit_from = unit_positions(old_heads, new_units)
    pick = (unit_from[:, None] == jnp.arange(UNITS, dtype=jnp.int32)[None, :]).astype(jnp.bfloat16)
    units_out = jnp.einsum(
        "rsxc,ux->rsuc",
        heads_out.reshape(rows_dev, STEPS, UNITS, HALF),
        pick,
        preferred_element_type=jnp.float32,
    ).astype(jnp.bfloat16)
    blocks = units_out.reshape(rows, devices, (UNITS // devices) * HALF).transpose(1, 0, 2)
    outputs_old = exchange(devices, blocks)
    flat_old = outputs_old.reshape(row_count, STEPS, (UNITS // devices) * HALF)
    return jnp.einsum(
        "ob,osc->bsc", to_old, flat_old, preferred_element_type=jnp.float32
    ).astype(jnp.bfloat16)


def solution(mesh):
    in_specs = (
        P("groups", None, None),
        P(("groups", "heads"), None),
        P(("groups", "heads"), None),
        P("groups", "heads"),
        P(("groups", "heads"), None, None, None),
        P(("groups", "heads"), None, None),
        P(),
        P(),
        P("groups"),
        P("groups"),
    )
    return jax.shard_map(
        on_device,
        mesh=mesh,
        in_specs=in_specs,
        out_specs=P("groups", None, "heads"),
        check_vma=False,
    )
```

```python
import functools

import jax
import jax.numpy as jnp
from jax import lax
from jax.experimental import pallas as pl
from jax.experimental.pallas import tpu as pltpu
from jax.sharding import PartitionSpec as P

H = 32
DK = 128
TAPS = 4
STEPS = 4
HALF = 64
UNITS = 64
CHANNELS = 3 * H * DK

GROUP = 4
SPAN = H * DK // GROUP
CHUNK = 256
PER_SPAN = SPAN // CHUNK
CHUNKS = 3 * PER_SPAN
LAG = 4

norm_eps = 1e-06


def project_kernel(
    devices,
    rows,
    w_ref,
    gate_ref,
    tap_ref,
    toks_ref,
    out_ref,
    gate_out_ref,
    tap_out_ref,
    land,
    partial,
    red,
    summed,
    final,
    gate_land,
    gate_partial,
    gate_red,
    tap_land,
    own_sem,
    w_send,
    w_recv,
    z_send,
    z_recv,
    f_send,
    f_recv,
    g_send,
    g_recv,
    h_send,
    h_recv,
    t_send,
    t_recv,
):
    me = lax.axis_index("heads")
    outer = devices // GROUP
    place, inner = me // GROUP, me % GROUP
    band = GROUP * rows

    def remote(src, dst, send, recv, target):
        return pltpu.make_async_remote_copy(
            src_ref=src,
            dst_ref=dst,
            send_sem=send,
            recv_sem=recv,
            device_id={"heads": target},
            device_id_type=pl.DeviceIdType.MESH,
        )

    def mate(k):
        return place * GROUP + (inner + k) % GROUP

    def across(k):
        return ((place + k) % outer) * GROUP + inner

    def source_columns(c, owner):
        start = (c // PER_SPAN) * H * DK + owner * SPAN + (c % PER_SPAN) * CHUNK
        return pl.ds(pl.multiple_of(start, CHUNK), CHUNK)

    def local_columns(c):
        return pl.ds(c * CHUNK, CHUNK)

    own = []
    for c in range(CHUNKS):
        own.append(
            pltpu.make_async_copy(
                w_ref.at[:, source_columns(c, inner)],
                land.at[0, :, local_columns(c)],
                own_sem.at[c],
            )
        )
        own[c].start()

    barrier = pltpu.get_barrier_semaphore()
    for k in range(1, devices):
        pl.semaphore_signal(
            barrier,
            inc=1,
            device_id={"heads": (me + k) % devices},
            device_id_type=pl.DeviceIdType.MESH,
        )
    pl.semaphore_wait(barrier, devices - 1)

    gates = []
    for k in range(1, GROUP):
        gates.append(
            remote(gate_ref, gate_land.at[k - 1], g_send.at[k - 1], g_recv.at[k - 1], mate(k))
        )
        gates[-1].start()
    spread = []
    for c in range(CHUNKS):
        group = []
        for k in range(1, GROUP):
            owner = (inner + k) % GROUP
            group.append(
                remote(
                    w_ref.at[:, source_columns(c, owner)],
                    land.at[k, :, local_columns(c)],
                    w_send.at[c, k - 1],
                    w_recv.at[c, k - 1],
                    mate(k),
                )
            )
            group[-1].start()
        spread.append(group)
    taps = []
    for k in range(1, devices):
        taps.append(
            remote(
                tap_ref, tap_land.at[me], t_send.at[k - 1], t_recv.at[k - 1], (me + k) % devices
            )
        )
        taps[-1].start()

    for copy in gates:
        copy.wait()
    total = jnp.dot(toks_ref[inner], gate_ref[...], preferred_element_type=jnp.float32)
    for k in range(1, GROUP):
        source = (inner + GROUP - k) % GROUP
        total = total + jnp.dot(
            toks_ref[source], gate_land[k - 1], preferred_element_type=jnp.float32
        )
    gate_partial[...] = total
    gate_sends = []
    for k in range(1, outer):
        start = ((place + k) % outer) * band + inner * rows
        gate_sends.append(
            remote(
                gate_partial.at[pl.ds(pl.multiple_of(start, rows), rows)],
                gate_red.at[k - 1],
                h_send.at[k - 1],
                h_recv.at[k - 1],
                across(k),
            )
        )
        gate_sends[-1].start()

    my_band = pl.ds(pl.multiple_of(place * band, band), band)
    crossing = []
    closing = []

    def finish(c):
        here = local_columns(c)
        for copy in crossing[c]:
            copy.wait()
        whole = partial[my_band, here]
        for k in range(1, outer):
            whole = whole + red[k - 1, :, here]
        summed[:, here] = whole
        group = []
        for k in range(1, GROUP):
            start = ((inner + k) % GROUP) * rows
            group.append(
                remote(
                    summed.at[pl.ds(pl.multiple_of(start, rows), rows), here],
                    final.at[k - 1, :, here],
                    f_send.at[c, k - 1],
                    f_recv.at[c, k - 1],
                    mate(k),
                )
            )
            group[-1].start()
        closing.append(group)

    for c in range(CHUNKS):
        here = local_columns(c)
        own[c].wait()
        for copy in spread[c]:
            copy.wait_recv()
        total = jnp.dot(toks_ref[inner], land[0, :, here], preferred_element_type=jnp.float32)
        for k in range(1, GROUP):
            source = (inner + GROUP - k) % GROUP
            total = total + jnp.dot(
                toks_ref[source], land[k, :, here], preferred_element_type=jnp.float32
            )
        partial[:, here] = total
        group = []
        for k in range(1, outer):
            start = ((place + k) % outer) * band
            group.append(
                remote(
                    partial.at[pl.ds(pl.multiple_of(start, band), band), here],
                    red.at[k - 1, :, here],
                    z_send.at[c, k - 1],
                    z_recv.at[c, k - 1],
                    across(k),
                )
            )
            group[-1].start()
        crossing.append(group)
        if c >= LAG:
            finish(c - LAG)
    for c in range(CHUNKS - LAG, CHUNKS):
        finish(c)

    for copy in gate_sends:
        copy.wait()
    my_rows = pl.ds(pl.multiple_of(me * rows, rows), rows)
    gate_total = gate_partial[my_rows, :]
    for k in range(1, outer):
        gate_total = gate_total + gate_red[k - 1]
    gate_out_ref[...] = gate_total
    for copy in taps:
        copy.wait()
    tap_land[me] = tap_ref[...]
    tap_out_ref[...] = tap_land[...]
    kept = pl.ds(pl.multiple_of(inner * rows, rows), rows)
    for c in range(CHUNKS):
        here = local_columns(c)
        out_ref[:, source_columns(c, inner)] = summed[kept, here]
        for k in range(1, GROUP):
            closing[c][k - 1].wait()
            source = (inner + GROUP - k) % GROUP
            out_ref[:, source_columns(c, source)] = final[k - 1, :, here]
    for group in spread:
        for copy in group:
            copy.wait_send()


def project(devices, rows, weight, gate, taps, toks):
    depth = weight.shape[0]
    outer = devices // GROUP
    total = devices * rows
    band = GROUP * rows
    dma = pltpu.SemaphoreType.DMA
    vmem = pl.BlockSpec(memory_space=pltpu.VMEM)
    return pl.pallas_call(
        functools.partial(project_kernel, devices, rows),
        out_shape=(
            jax.ShapeDtypeStruct((rows, CHANNELS), jnp.float32),
            jax.ShapeDtypeStruct((rows, gate.shape[1]), jnp.float32),
            jax.ShapeDtypeStruct((devices,) + taps.shape, taps.dtype),
        ),
        in_specs=[pl.BlockSpec(memory_space=pltpu.HBM), vmem, vmem, vmem],
        out_specs=(vmem, vmem, vmem),
        scratch_shapes=[
            pltpu.VMEM((GROUP, depth, 3 * SPAN), jnp.bfloat16),
            pltpu.VMEM((total, 3 * SPAN), jnp.float32),
            pltpu.VMEM((outer - 1, band, 3 * SPAN), jnp.float32),
            pltpu.VMEM((band, 3 * SPAN), jnp.float32),
            pltpu.VMEM((GROUP - 1, rows, 3 * SPAN), jnp.float32),
            pltpu.VMEM((GROUP - 1,) + gate.shape, jnp.bfloat16),
            pltpu.VMEM((total, gate.shape[1]), jnp.float32),
            pltpu.VMEM((outer - 1, rows, gate.shape[1]), jnp.float32),
            pltpu.VMEM((devices,) + taps.shape, taps.dtype),
            dma((CHUNKS,)),
            dma((CHUNKS, GROUP - 1)),
            dma((CHUNKS, GROUP - 1)),
            dma((CHUNKS, outer - 1)),
            dma((CHUNKS, outer - 1)),
            dma((CHUNKS, GROUP - 1)),
            dma((CHUNKS, GROUP - 1)),
            dma((GROUP - 1,)),
            dma((GROUP - 1,)),
            dma((outer - 1,)),
            dma((outer - 1,)),
            dma((devices - 1,)),
            dma((devices - 1,)),
        ],
        compiler_params=pltpu.CompilerParams(
            collective_id=0, has_side_effects=True, vmem_limit_bytes=48 * 1024 * 1024
        ),
    )(weight, gate, taps, toks)


def exchange_kernel(devices, blocks_ref, out_ref, land, send, recv):
    me = lax.axis_index("heads")
    barrier = pltpu.get_barrier_semaphore()
    for k in range(1, devices):
        pl.semaphore_signal(
            barrier,
            inc=1,
            device_id={"heads": (me + k) % devices},
            device_id_type=pl.DeviceIdType.MESH,
        )
    pl.semaphore_wait(barrier, devices - 1)
    copies = []
    for k in range(1, devices):
        target = (me + k) % devices
        copies.append(
            pltpu.make_async_remote_copy(
                src_ref=blocks_ref.at[target],
                dst_ref=land.at[me],
                send_sem=send.at[k - 1],
                recv_sem=recv.at[k - 1],
                device_id={"heads": target},
                device_id_type=pl.DeviceIdType.MESH,
            )
        )
        copies[-1].start()
    land[me] = blocks_ref[me]
    for copy in copies:
        copy.wait()
    out_ref[...] = land[...]


def exchange(devices, blocks):
    vmem = pl.BlockSpec(memory_space=pltpu.VMEM)
    return pl.pallas_call(
        functools.partial(exchange_kernel, devices),
        out_shape=jax.ShapeDtypeStruct(blocks.shape, blocks.dtype),
        in_specs=[vmem],
        out_specs=vmem,
        scratch_shapes=[
            pltpu.VMEM(blocks.shape, blocks.dtype),
            pltpu.SemaphoreType.DMA((devices - 1,)),
            pltpu.SemaphoreType.DMA((devices - 1,)),
        ],
        compiler_params=pltpu.CompilerParams(collective_id=1, has_side_effects=True),
    )(blocks)


def unit_positions(old_heads, new_units):
    positions = jnp.arange(H, dtype=jnp.int32)
    inverse = jnp.sum(
        jnp.where(old_heads[None, :] == positions[:, None], positions[None, :], 0), axis=1
    )
    heads_of = new_units // 2
    old_slots = jnp.sum(
        jnp.where(heads_of[:, None] == positions[None, :], inverse[None, :], 0), axis=1
    )
    return old_slots * 2 + new_units % 2


def normalize(values):
    return values * lax.rsqrt(jnp.sum(values * values, axis=-1, keepdims=True) + norm_eps)


def decode(projected, gate_pre, history, taps, state, live_lengths):
    rows = projected.shape[0]
    sequence = jnp.concatenate([history, projected], axis=1)
    weights_f = taps.astype(jnp.float32)
    convolved = weights_f[0][None, None] * sequence[:, 0:STEPS]
    for tap_index in range(1, TAPS):
        convolved = (
            convolved
            + weights_f[tap_index][None, None] * sequence[:, tap_index : tap_index + STEPS]
        )
    activated = jax.nn.silu(convolved).reshape(rows, STEPS, 3, H, DK)
    queries = normalize(activated[:, :, 0])
    keys = normalize(activated[:, :, 1])
    values = activated[:, :, 2]
    beta = jax.nn.sigmoid(gate_pre[:, :, 0])
    decay = jnp.exp(-jax.nn.softplus(gate_pre[:, :, 1]))
    both = jnp.concatenate([queries, keys], axis=1)
    based = jnp.einsum("rihk,rhkv->rihv", both, state, precision=lax.Precision.HIGH)
    query_base, key_base = based[:, :STEPS], based[:, STEPS:]

    corrections = []
    outs = []
    faded_base = jnp.ones_like(decay[:, 0])
    spans = []
    for s in range(STEPS):
        faded_base = faded_base * decay[:, s]
        spans = [span * decay[:, s] for span in spans]
        predicted = faded_base[..., None] * key_base[:, s]
        for j in range(s):
            overlap = jnp.sum(keys[:, s] * keys[:, j], axis=-1) * spans[j]
            predicted = predicted + overlap[..., None] * corrections[j]
        corrections.append(beta[:, s, :, None] * (values[:, s] - predicted))
        spans.append(jnp.ones_like(faded_base))
        now = faded_base[..., None] * query_base[:, s]
        for j in range(s + 1):
            overlap = jnp.sum(queries[:, s] * keys[:, j], axis=-1) * spans[j]
            now = now + overlap[..., None] * corrections[j]
        live = (s < live_lengths)[:, None, None]
        outs.append(jnp.where(live, now, jnp.zeros_like(now)))
    return jnp.stack(outs, axis=1).astype(jnp.bfloat16)


def on_device(
    tokens,
    qkv_weight,
    gate_weight,
    conv_weight,
    delta_state,
    conv_state,
    old_heads,
    new_units,
    slot_of,
    lengths,
):
    devices = lax.axis_size("heads")
    my_index = lax.axis_index("heads")
    row_count = tokens.shape[0]
    rows_dev = delta_state.shape[0]
    depth = qkv_weight.shape[0]
    row_range = jnp.arange(row_count, dtype=jnp.int32)
    to_old = (slot_of[None, :] == row_range[:, None]).astype(jnp.bfloat16)
    rows = rows_dev * STEPS
    place = my_index // GROUP
    my_tokens = lax.dynamic_slice_in_dim(tokens, place * GROUP * depth, GROUP * depth, 2)
    tokens_old = jnp.einsum(
        "ob,bsd->osd", to_old, my_tokens, preferred_element_type=jnp.float32
    ).astype(jnp.bfloat16)
    toks = tokens_old.reshape(row_count * STEPS, GROUP, depth).transpose(1, 0, 2)
    gate_padded = jnp.pad(gate_weight, ((0, 0), (0, 128 - 2 * H)))
    mine, gate_mine, tap_table = project(devices, rows, qkv_weight, gate_padded, conv_weight, toks)
    projected = mine.reshape(rows_dev, STEPS, CHANNELS)
    gate_pre = gate_mine[:, : 2 * H].reshape(rows_dev, STEPS, 2, H)
    taps = tap_table.transpose(1, 0, 2).reshape(TAPS, CHANNELS)

    my_slots = my_index * rows_dev + jnp.arange(rows_dev, dtype=jnp.int32)
    live_lengths = jnp.sum(
        jnp.where(slot_of[None, :] == my_slots[:, None], lengths[None, :], 0), axis=1
    )
    heads_out = decode(projected, gate_pre, conv_state, taps, delta_state, live_lengths)

    unit_from = unit_positions(old_heads, new_units)
    pick = (unit_from[:, None] == jnp.arange(UNITS, dtype=jnp.int32)[None, :]).astype(jnp.bfloat16)
    units_out = jnp.einsum(
        "rsxc,ux->rsuc",
        heads_out.reshape(rows_dev, STEPS, UNITS, HALF),
        pick,
        preferred_element_type=jnp.float32,
    ).astype(jnp.bfloat16)
    blocks = units_out.reshape(rows, devices, (UNITS // devices) * HALF).transpose(1, 0, 2)
    outputs_old = exchange(devices, blocks)
    flat_old = outputs_old.reshape(row_count, STEPS, (UNITS // devices) * HALF)
    return jnp.einsum(
        "ob,osc->bsc", to_old, flat_old, preferred_element_type=jnp.float32
    ).astype(jnp.bfloat16)


def solution(mesh):
    in_specs = (
        P("groups", None, None),
        P(("groups", "heads"), None),
        P(("groups", "heads"), None),
        P("groups", "heads"),
        P(("groups", "heads"), None, None, None),
        P(("groups", "heads"), None, None),
        P(),
        P(),
        P("groups"),
        P("groups"),
    )
    return jax.shard_map(
        on_device,
        mesh=mesh,
        in_specs=in_specs,
        out_specs=P("groups", None, "heads"),
        check_vma=False,
    )
```

```python
import functools

import jax
import jax.numpy as jnp
from jax import lax
from jax.experimental import pallas as pl
from jax.experimental.pallas import tpu as pltpu
from jax.sharding import PartitionSpec as P

H = 32
DK = 128
TAPS = 4
STEPS = 4
HALF = 64
UNITS = 64
CHANNELS = 3 * H * DK

GROUP = 4
SPAN = H * DK // GROUP
CHUNK = 256
PER_SPAN = SPAN // CHUNK
CHUNKS = 3 * PER_SPAN
LAG = 4

norm_eps = 1e-06


def project_kernel(
    devices,
    rows,
    w_ref,
    gate_ref,
    tap_ref,
    toks_ref,
    out_ref,
    gate_out_ref,
    tap_out_ref,
    land,
    partial,
    red,
    summed,
    final,
    gate_land,
    gate_partial,
    gate_red,
    tap_land,
    own_sem,
    w_send,
    w_recv,
    z_send,
    z_recv,
    f_send,
    f_recv,
    g_send,
    g_recv,
    h_send,
    h_recv,
    t_send,
    t_recv,
):
    me = lax.axis_index("heads")
    outer = devices // GROUP
    place, inner = me // GROUP, me % GROUP
    band = GROUP * rows

    def remote(src, dst, send, recv, target):
        return pltpu.make_async_remote_copy(
            src_ref=src,
            dst_ref=dst,
            send_sem=send,
            recv_sem=recv,
            device_id={"heads": target},
            device_id_type=pl.DeviceIdType.MESH,
        )

    def mate(k):
        return place * GROUP + (inner + k) % GROUP

    def across(k):
        return ((place + k) % outer) * GROUP + inner

    def source_columns(c, owner):
        start = (c // PER_SPAN) * H * DK + owner * SPAN + (c % PER_SPAN) * CHUNK
        return pl.ds(pl.multiple_of(start, CHUNK), CHUNK)

    def local_columns(c):
        return pl.ds(c * CHUNK, CHUNK)

    own = []
    for c in range(CHUNKS):
        own.append(
            pltpu.make_async_copy(
                w_ref.at[:, source_columns(c, inner)],
                land.at[0, :, local_columns(c)],
                own_sem.at[c],
            )
        )
        own[c].start()

    barrier = pltpu.get_barrier_semaphore()
    for k in range(1, devices):
        pl.semaphore_signal(
            barrier,
            inc=1,
            device_id={"heads": (me + k) % devices},
            device_id_type=pl.DeviceIdType.MESH,
        )
    pl.semaphore_wait(barrier, devices - 1)

    gates = []
    for k in range(1, GROUP):
        gates.append(
            remote(gate_ref, gate_land.at[k - 1], g_send.at[k - 1], g_recv.at[k - 1], mate(k))
        )
        gates[-1].start()
    spread = []
    for c in range(CHUNKS):
        group = []
        for k in range(1, GROUP):
            owner = (inner + k) % GROUP
            group.append(
                remote(
                    w_ref.at[:, source_columns(c, owner)],
                    land.at[k, :, local_columns(c)],
                    w_send.at[c, k - 1],
                    w_recv.at[c, k - 1],
                    mate(k),
                )
            )
            group[-1].start()
        spread.append(group)
    taps = []
    for k in range(1, devices):
        taps.append(
            remote(
                tap_ref, tap_land.at[me], t_send.at[k - 1], t_recv.at[k - 1], (me + k) % devices
            )
        )
        taps[-1].start()

    for copy in gates:
        copy.wait()
    total = jnp.dot(toks_ref[inner], gate_ref[...], preferred_element_type=jnp.float32)
    for k in range(1, GROUP):
        source = (inner + GROUP - k) % GROUP
        total = total + jnp.dot(
            toks_ref[source], gate_land[k - 1], preferred_element_type=jnp.float32
        )
    gate_partial[...] = total
    gate_sends = []
    for k in range(1, outer):
        start = ((place + k) % outer) * band + inner * rows
        gate_sends.append(
            remote(
                gate_partial.at[pl.ds(pl.multiple_of(start, rows), rows)],
                gate_red.at[k - 1],
                h_send.at[k - 1],
                h_recv.at[k - 1],
                across(k),
            )
        )
        gate_sends[-1].start()

    my_band = pl.ds(pl.multiple_of(place * band, band), band)
    crossing = []
    closing = []

    def finish(c):
        here = local_columns(c)
        for copy in crossing[c]:
            copy.wait()
        whole = partial[my_band, here]
        for k in range(1, outer):
            whole = whole + red[k - 1, :, here]
        summed[:, here] = whole
        group = []
        for k in range(1, GROUP):
            start = ((inner + k) % GROUP) * rows
            group.append(
                remote(
                    summed.at[pl.ds(pl.multiple_of(start, rows), rows), here],
                    final.at[k - 1, :, here],
                    f_send.at[c, k - 1],
                    f_recv.at[c, k - 1],
                    mate(k),
                )
            )
            group[-1].start()
        closing.append(group)

    for c in range(CHUNKS):
        here = local_columns(c)
        own[c].wait()
        for copy in spread[c]:
            copy.wait_recv()
        total = jnp.dot(toks_ref[inner], land[0, :, here], preferred_element_type=jnp.float32)
        for k in range(1, GROUP):
            source = (inner + GROUP - k) % GROUP
            total = total + jnp.dot(
                toks_ref[source], land[k, :, here], preferred_element_type=jnp.float32
            )
        partial[:, here] = total
        group = []
        for k in range(1, outer):
            start = ((place + k) % outer) * band
            group.append(
                remote(
                    partial.at[pl.ds(pl.multiple_of(start, band), band), here],
                    red.at[k - 1, :, here],
                    z_send.at[c, k - 1],
                    z_recv.at[c, k - 1],
                    across(k),
                )
            )
            group[-1].start()
        crossing.append(group)
        if c >= LAG:
            finish(c - LAG)
    for c in range(CHUNKS - LAG, CHUNKS):
        finish(c)

    for copy in gate_sends:
        copy.wait()
    my_rows = pl.ds(pl.multiple_of(me * rows, rows), rows)
    gate_total = gate_partial[my_rows, :]
    for k in range(1, outer):
        gate_total = gate_total + gate_red[k - 1]
    gate_out_ref[...] = gate_total
    for copy in taps:
        copy.wait()
    tap_land[me] = tap_ref[...]
    tap_out_ref[...] = tap_land[...]
    kept = pl.ds(pl.multiple_of(inner * rows, rows), rows)
    for c in range(CHUNKS):
        here = local_columns(c)
        out_ref[:, source_columns(c, inner)] = summed[kept, here]
        for k in range(1, GROUP):
            closing[c][k - 1].wait()
            source = (inner + GROUP - k) % GROUP
            out_ref[:, source_columns(c, source)] = final[k - 1, :, here]
    for group in spread:
        for copy in group:
            copy.wait_send()


def project(devices, rows, weight, gate, taps, toks):
    depth = weight.shape[0]
    outer = devices // GROUP
    total = devices * rows
    band = GROUP * rows
    dma = pltpu.SemaphoreType.DMA
    vmem = pl.BlockSpec(memory_space=pltpu.VMEM)
    return pl.pallas_call(
        functools.partial(project_kernel, devices, rows),
        out_shape=(
            jax.ShapeDtypeStruct((rows, CHANNELS), jnp.float32),
            jax.ShapeDtypeStruct((rows, gate.shape[1]), jnp.float32),
            jax.ShapeDtypeStruct((devices,) + taps.shape, taps.dtype),
        ),
        in_specs=[pl.BlockSpec(memory_space=pltpu.HBM), vmem, vmem, vmem],
        out_specs=(vmem, vmem, vmem),
        scratch_shapes=[
            pltpu.VMEM((GROUP, depth, 3 * SPAN), jnp.bfloat16),
            pltpu.VMEM((total, 3 * SPAN), jnp.float32),
            pltpu.VMEM((outer - 1, band, 3 * SPAN), jnp.float32),
            pltpu.VMEM((band, 3 * SPAN), jnp.float32),
            pltpu.VMEM((GROUP - 1, rows, 3 * SPAN), jnp.float32),
            pltpu.VMEM((GROUP - 1,) + gate.shape, jnp.bfloat16),
            pltpu.VMEM((total, gate.shape[1]), jnp.float32),
            pltpu.VMEM((outer - 1, rows, gate.shape[1]), jnp.float32),
            pltpu.VMEM((devices,) + taps.shape, taps.dtype),
            dma((CHUNKS,)),
            dma((CHUNKS, GROUP - 1)),
            dma((CHUNKS, GROUP - 1)),
            dma((CHUNKS, outer - 1)),
            dma((CHUNKS, outer - 1)),
            dma((CHUNKS, GROUP - 1)),
            dma((CHUNKS, GROUP - 1)),
            dma((GROUP - 1,)),
            dma((GROUP - 1,)),
            dma((outer - 1,)),
            dma((outer - 1,)),
            dma((devices - 1,)),
            dma((devices - 1,)),
        ],
        compiler_params=pltpu.CompilerParams(
            collective_id=0, has_side_effects=True, vmem_limit_bytes=61 * 1024 * 1024
        ),
    )(weight, gate, taps, toks)


def exchange_kernel(devices, blocks_ref, out_ref, land, send, recv):
    me = lax.axis_index("heads")
    barrier = pltpu.get_barrier_semaphore()
    for k in range(1, devices):
        pl.semaphore_signal(
            barrier,
            inc=1,
            device_id={"heads": (me + k) % devices},
            device_id_type=pl.DeviceIdType.MESH,
        )
    pl.semaphore_wait(barrier, devices - 1)
    copies = []
    for k in range(1, devices):
        target = (me + k) % devices
        copies.append(
            pltpu.make_async_remote_copy(
                src_ref=blocks_ref.at[target],
                dst_ref=land.at[me],
                send_sem=send.at[k - 1],
                recv_sem=recv.at[k - 1],
                device_id={"heads": target},
                device_id_type=pl.DeviceIdType.MESH,
            )
        )
        copies[-1].start()
    land[me] = blocks_ref[me]
    for copy in copies:
        copy.wait()
    out_ref[...] = land[...]


def exchange(devices, blocks):
    vmem = pl.BlockSpec(memory_space=pltpu.VMEM)
    return pl.pallas_call(
        functools.partial(exchange_kernel, devices),
        out_shape=jax.ShapeDtypeStruct(blocks.shape, blocks.dtype),
        in_specs=[vmem],
        out_specs=vmem,
        scratch_shapes=[
            pltpu.VMEM(blocks.shape, blocks.dtype),
            pltpu.SemaphoreType.DMA((devices - 1,)),
            pltpu.SemaphoreType.DMA((devices - 1,)),
        ],
        compiler_params=pltpu.CompilerParams(collective_id=1, has_side_effects=True),
    )(blocks)


def unit_positions(old_heads, new_units):
    positions = jnp.arange(H, dtype=jnp.int32)
    inverse = jnp.sum(
        jnp.where(old_heads[None, :] == positions[:, None], positions[None, :], 0), axis=1
    )
    heads_of = new_units // 2
    old_slots = jnp.sum(
        jnp.where(heads_of[:, None] == positions[None, :], inverse[None, :], 0), axis=1
    )
    return old_slots * 2 + new_units % 2


def normalize(values):
    return values * lax.rsqrt(jnp.sum(values * values, axis=-1, keepdims=True) + norm_eps)


def decode(projected, gate_pre, history, taps, state, live_lengths):
    rows = projected.shape[0]
    sequence = jnp.concatenate([history, projected], axis=1)
    weights_f = taps.astype(jnp.float32)
    convolved = weights_f[0][None, None] * sequence[:, 0:STEPS]
    for tap_index in range(1, TAPS):
        convolved = (
            convolved
            + weights_f[tap_index][None, None] * sequence[:, tap_index : tap_index + STEPS]
        )
    activated = jax.nn.silu(convolved).reshape(rows, STEPS, 3, H, DK)
    queries = normalize(activated[:, :, 0])
    keys = normalize(activated[:, :, 1])
    values = activated[:, :, 2]
    beta = jax.nn.sigmoid(gate_pre[:, :, 0])
    decay = jnp.exp(-jax.nn.softplus(gate_pre[:, :, 1]))
    both = jnp.concatenate([queries, keys], axis=1)
    based = jnp.einsum("rihk,rhkv->rihv", both, state, precision=lax.Precision.HIGH)
    query_base, key_base = based[:, :STEPS], based[:, STEPS:]

    corrections = []
    outs = []
    faded_base = jnp.ones_like(decay[:, 0])
    spans = []
    for s in range(STEPS):
        faded_base = faded_base * decay[:, s]
        spans = [span * decay[:, s] for span in spans]
        predicted = faded_base[..., None] * key_base[:, s]
        for j in range(s):
            overlap = jnp.sum(keys[:, s] * keys[:, j], axis=-1) * spans[j]
            predicted = predicted + overlap[..., None] * corrections[j]
        corrections.append(beta[:, s, :, None] * (values[:, s] - predicted))
        spans.append(jnp.ones_like(faded_base))
        now = faded_base[..., None] * query_base[:, s]
        for j in range(s + 1):
            overlap = jnp.sum(queries[:, s] * keys[:, j], axis=-1) * spans[j]
            now = now + overlap[..., None] * corrections[j]
        live = (s < live_lengths)[:, None, None]
        outs.append(jnp.where(live, now, jnp.zeros_like(now)))
    return jnp.stack(outs, axis=1).astype(jnp.bfloat16)


def on_device(
    tokens,
    qkv_weight,
    gate_weight,
    conv_weight,
    delta_state,
    conv_state,
    old_heads,
    new_units,
    slot_of,
    lengths,
):
    devices = lax.axis_size("heads")
    my_index = lax.axis_index("heads")
    row_count = tokens.shape[0]
    rows_dev = delta_state.shape[0]
    depth = qkv_weight.shape[0]
    row_range = jnp.arange(row_count, dtype=jnp.int32)
    to_old = (slot_of[None, :] == row_range[:, None]).astype(jnp.bfloat16)
    rows = rows_dev * STEPS
    place = my_index // GROUP
    my_tokens = lax.dynamic_slice_in_dim(tokens, place * GROUP * depth, GROUP * depth, 2)
    tokens_old = jnp.einsum(
        "ob,bsd->osd", to_old, my_tokens, preferred_element_type=jnp.float32
    ).astype(jnp.bfloat16)
    toks = tokens_old.reshape(row_count * STEPS, GROUP, depth).transpose(1, 0, 2)
    gate_padded = jnp.pad(gate_weight, ((0, 0), (0, 128 - 2 * H)))
    mine, gate_mine, tap_table = project(devices, rows, qkv_weight, gate_padded, conv_weight, toks)
    projected = mine.reshape(rows_dev, STEPS, CHANNELS)
    gate_pre = gate_mine[:, : 2 * H].reshape(rows_dev, STEPS, 2, H)
    taps = tap_table.transpose(1, 0, 2).reshape(TAPS, CHANNELS)

    my_slots = my_index * rows_dev + jnp.arange(rows_dev, dtype=jnp.int32)
    live_lengths = jnp.sum(
        jnp.where(slot_of[None, :] == my_slots[:, None], lengths[None, :], 0), axis=1
    )
    heads_out = decode(projected, gate_pre, conv_state, taps, delta_state, live_lengths)

    unit_from = unit_positions(old_heads, new_units)
    pick = (unit_from[:, None] == jnp.arange(UNITS, dtype=jnp.int32)[None, :]).astype(jnp.bfloat16)
    units_out = jnp.einsum(
        "rsxc,ux->rsuc",
        heads_out.reshape(rows_dev, STEPS, UNITS, HALF),
        pick,
        preferred_element_type=jnp.float32,
    ).astype(jnp.bfloat16)
    blocks = units_out.reshape(rows, devices, (UNITS // devices) * HALF).transpose(1, 0, 2)
    outputs_old = exchange(devices, blocks)
    flat_old = outputs_old.reshape(row_count, STEPS, (UNITS // devices) * HALF)
    return jnp.einsum(
        "ob,osc->bsc", to_old, flat_old, preferred_element_type=jnp.float32
    ).astype(jnp.bfloat16)


def solution(mesh):
    in_specs = (
        P("groups", None, None),
        P(("groups", "heads"), None),
        P(("groups", "heads"), None),
        P("groups", "heads"),
        P(("groups", "heads"), None, None, None),
        P(("groups", "heads"), None, None),
        P(),
        P(),
        P("groups"),
        P("groups"),
    )
    return jax.shard_map(
        on_device,
        mesh=mesh,
        in_specs=in_specs,
        out_specs=P("groups", None, "heads"),
        check_vma=False,
    )
```
